32 devices in a mesh: dp: 8 (over y, x, core), tensor: 4 (over z).
Axes of the slice: x: 2, y: 2, z: 4, core: 2. Of those that a mesh axis runs over, the one named last changes fastest.
Arguments:
- block_input: bfloat16 [2048, 2048], P('dp'), may hold values from -6 to 6
- segment_ids: int32 [8, 256], P('dp'), may hold values from 0 to 2, never falling along the last dimension, each value on 1 to 192 neighbouring positions
- expert_ids: int32 [2048, 8], P('dp'), may hold values from 0 to 31, all different within a row; in each aligned block of 256 rows (0 to 255, 256 to 511, ...) at most 128 rows name the same one
- attn_gain: float32 [2048], replicated, may hold values from 0.25 to 1.75
- query_weight: bfloat16 [2048, 4096], P(None, 'tensor'), may hold values from -0.125 to 0.125
- key_projection: bfloat16 [2048, 512], P(None, 'tensor'), may hold values from -0.125 to 0.125
- value_projection: bfloat16 [2048, 512], P(None, 'tensor'), may hold values from -0.125 to 0.125
- query_norm_gain: float32 [128], replicated, may hold values from 0.25 to 1.75
- key_norm_gain: float32 [128], replicated, may hold values from 0.25 to 1.75
- output_projection: bfloat16 [2048, 4096], P(None, 'tensor'), may hold values from -0.375 to 0.375
- ffn_gain: float32 [2048], replicated, may hold values from 0.25 to 1.75
- router_weight: bfloat16 [2048, 32], replicated, may hold values from -0.0625 to 0.0625
- gate_experts: bfloat16 [32, 2048, 768], P('dp', None, 'tensor'), may hold values from -0.125 to 0.125
- up_experts: bfloat16 [32, 2048, 768], P('dp', None, 'tensor'), may hold values from -0.125 to 0.125
- down_experts: bfloat16 [32, 768, 2048], P('dp', 'tensor'), may hold values from -0.4375 to 0.4375
- out_grad: bfloat16 [2048, 2048], P('dp'), may hold values from -6 to 6
Outputs:
- block_output: bfloat16 [2048, 2048], P('dp')
- input_grad: bfloat16 [2048, 2048], P('dp')
- attn_gain_grad: float32 [2048], P('dp')
- query_weight_grad: float32 [2048, 4096], P('dp', 'tensor')
- key_weight_grad: float32 [2048, 512], P('dp', 'tensor')
- value_weight_grad: float32 [2048, 512], P('dp', 'tensor')
- query_gain_grad: float32 [128], P('dp')
- key_gain_grad: float32 [128], P('dp')
- out_weight_grad: float32 [2048, 4096], P('dp', 'tensor')
- ffn_gain_grad: float32 [2048], P('dp')
- router_weight_grad: float32 [2048, 32], P('dp')
- gate_experts_grad: float32 [32, 2048, 768], P('dp', None, 'tensor')
- up_experts_grad: float32 [32, 2048, 768], P('dp', None, 'tensor')
- down_experts_grad: float32 [32, 768, 2048], P('dp', 'tensor')
The draws below stay inside these ranges and needn't reach their ends.
Inputs may be any that keep to these rules, and one draw needn't show every extreme that they name: `segment_ids`: segment ids never fall along a row; each segment holds 1 to 192 tokens and one of each row holds exactly 192. `expert_ids`: each row names 8 different experts. No expert is named by more than 128 of the rows of one index of dp, a bound that some block reaches by the rows of some index of dp.
All inputs are finite; a program needn't handle non-finite values.
Results may differ from the reference program's by a relative error of at most 0.03.
Values may be sent and summed in bfloat16 or wider, within the bound.
No kernel may reach another device: no remote copies, remote signals or barrier semaphores. Data moves between devices by JAX's collectives and lax.ppermute only.
A program may use at most 320 MiB of HBM per device.

```python
import math
import jax
import jax.numpy as jnp
import numpy as np
from jax import lax

MODEL_DIMENSION = 2048
QUERY_HEADS = 32
KEY_VALUE_HEADS = 4
HEAD_SIZE = 128
FF = 768
TOPK = 8
EXPERT_TOTAL = 32
TOKENS_PER_SHARD = 256
SEG_COUNT = 3
SEG_MOST = 192
TOKENS = 2048
CAP = 128
N_DP = 8
N_TENSOR = 4


def strengthened(values, stream_key, source, target, parts, factor):
    owner, partner = [(jnp.arange(values.shape[position]) // (values.shape[position] // parts)).reshape([-1 if axis == position else 1 for axis in range(values.ndim)]) for position in (source, target)]
    chosen = jax.random.permutation(stream_key, parts)[partner]
    strong = (owner == chosen) | (owner == (partner + parts // 2) % parts)
    return jnp.where(strong, factor * values, values)


def shard_levels(own_key, extent, cuts, smallest, largest):
    def one(dim, parts):
        heights = jax.random.uniform(jax.random.fold_in(jax.random.fold_in(own_key, 6), dim), (parts,), jnp.float32, smallest / len(cuts), largest / len(cuts))
        return jnp.repeat(jnp.exp(heights), extent[dim] // parts).reshape((-1,) + (1,) * (len(extent) - dim - 1))

    level = one(*cuts[0])
    for cut in cuts[1:]:
        level = level * one(*cut)
    return level


def length_profile(number_of, total, bound, lean):
    loads = [(1 << 20) // math.isqrt(rank ** lean) + 1 for rank in range(2, number_of + 1)]
    rest, given = total - bound - (number_of - 1), [1] * (number_of - 1)
    while rest > 0:
        candidates = [i for i in range(number_of - 1) if given[i] < bound]
        pool, left = sum([loads[i] for i in candidates]), rest
        for i in candidates:
            addition = min(bound - given[i], max(1, left * loads[i] // pool), rest)
            given[i] = given[i] + addition
            rest = rest - addition
    return np.array([bound] + given)


def uneven(own_key, number_of, total, reach, lean):
    if number_of == 2:
        one = jax.random.randint(own_key, (), max(1, total - reach), min(reach, total - 1) + 1)
        return jnp.stack([one, total - one])
    tallies = jnp.asarray(length_profile(number_of, total, reach, lean), jnp.int32)
    pairs = (number_of - 1) // 2
    source_of, taker = tallies[1:1 + 2 * pairs:2], tallies[2:2 + 2 * pairs:2]
    room = jnp.minimum(source_of - 1, reach - taker)
    moved = jax.random.randint(jax.random.fold_in(own_key, 1), (pairs,), 0, 1 << 20) % (room + 1)
    tallies = tallies.at[1:1 + 2 * pairs:2].set(source_of - moved).at[2:2 + 2 * pairs:2].set(taker + moved)
    return tallies[jax.random.permutation(jax.random.fold_in(own_key, 2), number_of)]


def routed_block(key, own, number, rows, number_of, top, most, slope):
    sequence = jax.random.permutation(key, number_of)
    crowded, common = shares(number_of, rows * top, most, slope, True), shares(number_of, rows * top, most, slope, False)
    places = jnp.arange(number_of)

    def named(tallies, rotation):
        used = int((tallies > 0).sum())
        fixed = max(1, used // 4)
        passed = fixed + (places - fixed + rotation * (used - fixed)) % max(1, number_of - fixed)
        return jnp.zeros((number_of,), jnp.int32).at[sequence[jnp.where(places < fixed, places, passed)]].set(jnp.asarray(tallies, jnp.int32))

    tallies = jnp.where(number % 4 == 0, named(crowded, number // 4), named(common, number - number // 4 - 1))
    mixed = jax.random.permutation(jax.random.fold_in(own, 3), number_of)
    donor, taker = mixed[0:number_of // 2 * 2:2], mixed[1:number_of // 2 * 2:2]
    room = jnp.minimum(tallies[donor] - 1, most - tallies[taker]) // 2
    room = jnp.where((donor == sequence[0]) | (taker == sequence[0]) | (tallies[taker] == 0), 0, jnp.maximum(room, 0))
    passed = jax.random.randint(jax.random.fold_in(own, 4), (number_of // 2,), 0, 1 << 20) % (room + 1)
    tallies = tallies.at[donor].add(-passed).at[taker].add(passed)
    items = jnp.searchsorted(jnp.cumsum(tallies), jnp.arange(rows * top), side="right").astype(jnp.int32)
    grid = items.reshape(top, rows).T
    grid = grid[jax.random.permutation(jax.random.fold_in(own, 1), rows)]
    rotation = jax.random.randint(jax.random.fold_in(own, 2), (rows, 1), 0, top)
    return jnp.take_along_axis(grid, (jnp.arange(top)[None, :] + rotation) % top, axis=1)


def shares(count, total, limit, lean, full):
    loads = [(1 << 20) // math.isqrt(rank ** lean) + 1 for rank in range(1, count + 1)]
    largest = limit if full else min(limit, max(-(-total // count), total * loads[0] // sum(loads)))
    least = 1 if total - largest >= count - 1 else 0
    given, spare = [largest] + [least] * (count - 1), total - largest - least * (count - 1)
    while spare > 0:
        free = [i for i in range(1, count) if given[i] < largest] or [i for i in range(1, count) if given[i] < limit]
        mass, budget = sum([loads[i] for i in free]), spare
        for i in free:
            addition = min(limit - given[i], max(1, budget * loads[i] // mass), spare)
            given[i] = given[i] + addition
            spare = spare - addition
    return np.array(given)


def scatter_about(rng, extent, width, most, cuts=(), held_as=jnp.bfloat16):
    array = width * jax.random.normal(rng, extent, jnp.float32)
    if cuts:
        array = array * shard_levels(rng, extent, cuts, -0.22, 0.18)
    return jnp.clip(array, -most, most).astype(held_as)


def gaussian_with(own_key, extent, width, reach, cuts, heavy, held_as=jnp.bfloat16):
    entries = width * jax.random.normal(own_key, extent, jnp.float32)
    if cuts:
        entries = entries * shard_levels(own_key, extent, cuts, -0.22, 0.18)
    return jnp.clip(strengthened(entries, jax.random.fold_in(own_key, 3), *heavy), -reach, reach).astype(held_as)


def setup_inputs(seed: int = 0) -> dict:
    key_list = jax.random.split(jax.random.key(seed), 17)
    block_input = scatter_about(key_list[0], (TOKENS, MODEL_DIMENSION), 1.0, 6.0, ((0, 8),))
    segment_ids = jax.vmap(lambda own: jnp.searchsorted(jnp.cumsum(uneven(own, SEG_COUNT, TOKENS_PER_SHARD, SEG_MOST, 2)), jnp.arange(TOKENS_PER_SHARD), side="right"))(jax.random.split(key_list[1], N_DP)).reshape((N_DP, TOKENS_PER_SHARD)).astype(jnp.int32)
    expert_ids_keys = jax.random.split(jax.random.fold_in(key_list[2], 1), TOKENS // TOKENS_PER_SHARD)
    expert_ids_turns = jax.random.permutation(jax.random.fold_in(key_list[2], 3), TOKENS // TOKENS_PER_SHARD)
    expert_ids = jax.vmap(lambda own, number: routed_block(jax.random.fold_in(key_list[2], 2), own, number, TOKENS_PER_SHARD, EXPERT_TOTAL, TOPK, CAP, 2))(expert_ids_keys, expert_ids_turns).reshape((TOKENS, TOPK))
    attn_gain = jnp.clip(1.0 + 0.15 * jax.random.normal(key_list[3], (MODEL_DIMENSION,), jnp.float32), 0.25, 1.75)
    query_weight = scatter_about(key_list[4], (MODEL_DIMENSION, QUERY_HEADS * HEAD_SIZE), MODEL_DIMENSION ** -0.5, 0.125, ((1, 4),))
    key_projection = scatter_about(key_list[5], (MODEL_DIMENSION, KEY_VALUE_HEADS * HEAD_SIZE), MODEL_DIMENSION ** -0.5, 0.125, ((1, 4),))
    value_projection = scatter_about(key_list[6], (MODEL_DIMENSION, KEY_VALUE_HEADS * HEAD_SIZE), MODEL_DIMENSION ** -0.5, 0.125, ((1, 4),))
    query_norm_gain = jnp.clip(1.0 + 0.15 * jax.random.normal(key_list[7], (HEAD_SIZE,), jnp.float32), 0.25, 1.75)
    key_norm_gain = jnp.clip(1.0 + 0.15 * jax.random.normal(key_list[8], (HEAD_SIZE,), jnp.float32), 0.25, 1.75)
    output_projection = scatter_about(key_list[9], (MODEL_DIMENSION, QUERY_HEADS * HEAD_SIZE), (QUERY_HEADS * HEAD_SIZE // 16) ** -0.5, 0.375, ((1, 4),))
    ffn_gain = jnp.clip(1.0 + 0.15 * jax.random.normal(key_list[10], (MODEL_DIMENSION,), jnp.float32), 0.25, 1.75)
    router_weight = scatter_about(key_list[11], (MODEL_DIMENSION, EXPERT_TOTAL), (MODEL_DIMENSION * 4) ** -0.5, 0.0625)
    gate_experts = scatter_about(key_list[12], (EXPERT_TOTAL, MODEL_DIMENSION, FF), MODEL_DIMENSION ** -0.5, 0.125, ((0, 8), (2, 4)))
    up_experts = scatter_about(key_list[13], (EXPERT_TOTAL, MODEL_DIMENSION, FF), MODEL_DIMENSION ** -0.5, 0.125, ((0, 8), (2, 4)))
    down_experts = scatter_about(key_list[14], (EXPERT_TOTAL, FF, MODEL_DIMENSION), (FF // 4) ** -0.5, 0.4375, ((0, 8), (1, 4)))
    out_grad = gaussian_with(key_list[15], (TOKENS, MODEL_DIMENSION), 1.0, 6.0, ((0, 8),), (0, 1, 8, 2.0))
    return {"block_input": block_input, "segment_ids": segment_ids, "expert_ids": expert_ids, "attn_gain": attn_gain, "query_weight": query_weight, "key_projection": key_projection, "value_projection": value_projection, "query_norm_gain": query_norm_gain, "key_norm_gain": key_norm_gain, "output_projection": output_projection, "ffn_gain": ffn_gain, "router_weight": router_weight, "gate_experts": gate_experts, "up_experts": up_experts, "down_experts": down_experts, "out_grad": out_grad}


EPS = 1e-06
THETA = 1000000.0

def widen(value_tensor):
    return lax.optimization_barrier(value_tensor).astype(jnp.float32)

def rms_scale(value_tensor):
    return lax.rsqrt(lax.optimization_barrier(jnp.mean(value_tensor * value_tensor, axis=-1, keepdims=True)) + EPS)

def norm_reverse(grad_rows, normed, scale_rows):
    return scale_rows * (grad_rows - normed * lax.optimization_barrier(jnp.mean(grad_rows * normed, axis=-1, keepdims=True)))

def rope_tables(segment_row):
    index_row = jnp.arange(TOKENS_PER_SHARD, dtype=jnp.int32)
    same_seg = segment_row[:, None] == segment_row[None, :]
    before = index_row[None, :] < index_row[:, None]
    positions = lax.optimization_barrier(jnp.sum((same_seg & before).astype(jnp.int32), axis=1))
    half_dim = HEAD_SIZE // 2
    frequency = THETA ** (-(jnp.arange(half_dim, dtype=jnp.float32) * 2.0) / HEAD_SIZE)
    angles = positions.astype(jnp.float32)[:, None] * frequency[None, :]
    return (jnp.cos(angles), jnp.sin(angles))

def apply_rotation(value_tensor, cosine_table, sine_lookup):
    half_dim = value_tensor.shape[-1] // 2
    low_half = value_tensor[..., :half_dim]
    high_half = value_tensor[..., half_dim:]
    cos_rows = cosine_table[:, None, :]
    sin_rows = sine_lookup[:, None, :]
    return jnp.concatenate([low_half * cos_rows - high_half * sin_rows, high_half * cos_rows + low_half * sin_rows], axis=-1)

def rotate_back(grad_rows, cosine_table, sine_lookup):
    half_dim = grad_rows.shape[-1] // 2
    low_half = grad_rows[..., :half_dim]
    high_half = grad_rows[..., half_dim:]
    cos_rows = cosine_table[:, None, :]
    sin_rows = sine_lookup[:, None, :]
    return jnp.concatenate([low_half * cos_rows + high_half * sin_rows, high_half * cos_rows - low_half * sin_rows], axis=-1)

def attention_pieces(x_rows, segment_row, attn_gain, query_weight, key_projection, value_projection, query_norm_gain, key_norm_gain, output_projection):
    group_width = QUERY_HEADS // KEY_VALUE_HEADS
    inputs_f = x_rows.astype(jnp.float32)
    scale_one = rms_scale(inputs_f)
    normed_one = inputs_f * scale_one
    attention_input = (normed_one * attn_gain).astype(jnp.bfloat16)
    cosine_table, sine_lookup = rope_tables(segment_row)
    query_raw = jnp.dot(attention_input, query_weight, preferred_element_type=jnp.float32).reshape(TOKENS_PER_SHARD, QUERY_HEADS, HEAD_SIZE)
    query_scale = rms_scale(query_raw)
    query_normalized = query_raw * query_scale
    query_rotated = apply_rotation(query_normalized * query_norm_gain, cosine_table, sine_lookup).astype(jnp.bfloat16).reshape(TOKENS_PER_SHARD, KEY_VALUE_HEADS, group_width, HEAD_SIZE)
    key_unnormed = jnp.dot(attention_input, key_projection, preferred_element_type=jnp.float32).reshape(TOKENS_PER_SHARD, KEY_VALUE_HEADS, HEAD_SIZE)
    key_norm_scale = rms_scale(key_unnormed)
    key_normalized = key_unnormed * key_norm_scale
    key_rot = apply_rotation(key_normalized * key_norm_gain, cosine_table, sine_lookup).astype(jnp.bfloat16)
    value_row_block = jnp.dot(attention_input, value_projection, preferred_element_type=jnp.float32).astype(jnp.bfloat16).reshape(TOKENS_PER_SHARD, KEY_VALUE_HEADS, HEAD_SIZE)
    index_row = jnp.arange(TOKENS_PER_SHARD, dtype=jnp.int32)
    allowed = (segment_row[:, None] == segment_row[None, :]) & (index_row[None, :] <= index_row[:, None])
    scores = jnp.einsum('qkgd,skd->kgqs', widen(query_rotated), widen(key_rot)) * HEAD_SIZE ** (-0.5)
    scores = jnp.where(allowed, scores, -jnp.inf)
    top_score = lax.optimization_barrier(jnp.max(scores, axis=-1, keepdims=True))
    weights = jnp.exp(scores - top_score)
    totals = lax.optimization_barrier(jnp.sum(weights, axis=-1, keepdims=True))
    prob_rows = (weights / totals).astype(jnp.bfloat16)
    attn_out = jnp.einsum('kgqs,skd->qkgd', widen(prob_rows), widen(value_row_block)).astype(jnp.bfloat16)
    log_sums = top_score + jnp.log(totals)
    attn_flat = attn_out.reshape(TOKENS_PER_SHARD, QUERY_HEADS * HEAD_SIZE)
    attn_total = jnp.dot(attn_flat, output_projection.T, preferred_element_type=jnp.float32)
    middle = inputs_f + attn_total
    scale_two = rms_scale(middle)
    normed_two = middle * scale_two
    return {'scale_one': scale_one, 'normed_one': normed_one, 'attn_in': attention_input, 'cosine': cosine_table, 'sine_table': sine_lookup, 'query_scale': query_scale, 'query_hat': query_normalized, 'query_rot': query_rotated, 'key_scale': key_norm_scale, 'key_hat': key_normalized, 'key_rot': key_rot, 'value_rows': value_row_block, 'scores': scores, 'log_sums': log_sums, 'attn_out': attn_out, 'attn_flat': attn_flat, 'middle': middle, 'scale_two': scale_two, 'normed_two': normed_two}

def reference(block_input, segment_ids, expert_ids, attn_gain, query_weight, key_projection, value_projection, query_norm_gain, key_norm_gain, output_projection, ffn_gain, router_weight, gate_experts, up_experts, down_experts, out_grad):
    group_width = QUERY_HEADS // KEY_VALUE_HEADS
    input_dev = block_input.reshape(N_DP, TOKENS_PER_SHARD, MODEL_DIMENSION)
    grad_dev = out_grad.reshape(N_DP, TOKENS_PER_SHARD, MODEL_DIMENSION)

    def forward_device(pair_rows):
        x_rows, segment_row = pair_rows
        piece_list = attention_pieces(x_rows, segment_row, attn_gain, query_weight, key_projection, value_projection, query_norm_gain, key_norm_gain, output_projection)
        ffn_in = (piece_list['normed_two'] * ffn_gain).astype(jnp.bfloat16)
        return (piece_list['middle'], ffn_in)
    middle_all, ffn_all = lax.map(forward_device, (input_dev, segment_ids))
    ids_dev = expert_ids.reshape(N_DP, TOKENS_PER_SHARD, TOPK)
    logits = jnp.dot(ffn_all.reshape(TOKENS, MODEL_DIMENSION), router_weight, preferred_element_type=jnp.float32).reshape(N_DP, TOKENS_PER_SHARD, EXPERT_TOTAL)
    logit_exp = jnp.exp(logits - lax.optimization_barrier(jnp.max(logits, axis=-1, keepdims=True)))
    router_prob = logit_exp / lax.optimization_barrier(jnp.sum(logit_exp, axis=-1, keepdims=True))
    choose_hot = ids_dev[..., None] == jnp.arange(EXPERT_TOTAL, dtype=jnp.int32)
    choose_int = choose_hot.astype(jnp.int32)
    choose_float = choose_hot.astype(jnp.float32)
    selected = lax.optimization_barrier(jnp.sum(choose_float * router_prob[:, :, None, :], axis=3))
    gate_values = selected / lax.optimization_barrier(jnp.sum(selected, axis=-1, keepdims=True))
    member = lax.optimization_barrier(jnp.sum(choose_int, axis=2))
    earlier = jnp.cumsum(member, axis=1) - member
    slot_pos = lax.optimization_barrier(jnp.sum(choose_int * earlier[:, :, None, :], axis=3))
    slot_index = (ids_dev * CAP + slot_pos).astype(jnp.int32)
    device_rows = jnp.broadcast_to(jnp.arange(N_DP, dtype=jnp.int32)[:, None, None], slot_index.shape)
    token_rows = jnp.broadcast_to(jnp.arange(TOKENS_PER_SHARD, dtype=jnp.int32)[None, :, None], slot_index.shape)
    slot_token = jnp.full((N_DP, EXPERT_TOTAL * CAP), -1, jnp.int32).at[device_rows, slot_index].set(token_rows)
    slot_gate = jnp.zeros((N_DP, EXPERT_TOTAL * CAP), jnp.float32).at[device_rows, slot_index].set(gate_values)
    device_col = jnp.arange(N_DP, dtype=jnp.int32)[:, None]
    part_ff = FF // N_TENSOR

    def expert_step(carry, expert_inputs):
        mix_sum, back_sum = carry
        expert_index, weight_gate, weight_up, weight_down = expert_inputs
        tokens_here = lax.dynamic_slice_in_dim(slot_token, expert_index * CAP, CAP, 1)
        gates_here = lax.dynamic_slice_in_dim(slot_gate, expert_index * CAP, CAP, 1)
        is_valid = tokens_here >= 0
        safe_rows = jnp.maximum(tokens_here, 0)
        rows_in = jnp.where(is_valid[..., None], ffn_all[device_col, safe_rows], jnp.zeros((), jnp.bfloat16))
        gate_pre = jnp.einsum('scd,df->scf', widen(rows_in), widen(weight_gate))
        up_pre = jnp.einsum('scd,df->scf', widen(rows_in), widen(weight_up))
        activated = jax.nn.silu(gate_pre)
        hidden = (activated * up_pre).astype(jnp.bfloat16)
        hidden_split = widen(hidden).reshape(N_DP, CAP, N_TENSOR, part_ff)
        down_split = widen(weight_down).reshape(N_TENSOR, part_ff, MODEL_DIMENSION)
        partial_out = jnp.einsum('sctf,tfd->sctd', hidden_split, down_split).astype(jnp.bfloat16)
        expert_out = lax.optimization_barrier(jnp.sum(widen(partial_out), axis=2)).astype(jnp.bfloat16)
        out_wide = widen(expert_out)
        mix_sum = mix_sum.at[device_col, safe_rows].add(gates_here[..., None] * out_wide)
        grad_in = jnp.where(is_valid[..., None], grad_dev[device_col, safe_rows], jnp.zeros((), jnp.bfloat16))
        gate_dot = lax.optimization_barrier(jnp.sum(grad_in.astype(jnp.float32) * out_wide, axis=-1))
        slot_grad = (gates_here[..., None] * grad_in.astype(jnp.float32)).astype(jnp.bfloat16)
        hidden_grad = jnp.einsum('scd,fd->scf', widen(slot_grad), widen(weight_down))
        sigmoid_gate = jax.nn.sigmoid(gate_pre)
        gate_pre_grad = (hidden_grad * up_pre * sigmoid_gate * (1.0 + gate_pre * (1.0 - sigmoid_gate))).astype(jnp.bfloat16)
        up_pre_grad = (hidden_grad * activated).astype(jnp.bfloat16)
        down_w_grad = jnp.einsum('scf,scd->fd', widen(hidden), widen(slot_grad))
        gate_w_grad = jnp.einsum('scd,scf->df', widen(rows_in), widen(gate_pre_grad))
        up_w_grad = jnp.einsum('scd,scf->df', widen(rows_in), widen(up_pre_grad))
        gate_split = widen(gate_pre_grad).reshape(N_DP, CAP, N_TENSOR, part_ff)
        up_split = widen(up_pre_grad).reshape(N_DP, CAP, N_TENSOR, part_ff)
        wg_split = widen(weight_gate).reshape(MODEL_DIMENSION, N_TENSOR, part_ff)
        wu_split = widen(weight_up).reshape(MODEL_DIMENSION, N_TENSOR, part_ff)
        back_parts = (jnp.einsum('sctf,dtf->sctd', gate_split, wg_split) + jnp.einsum('sctf,dtf->sctd', up_split, wu_split)).astype(jnp.bfloat16)
        back_rows = lax.optimization_barrier(jnp.sum(widen(back_parts), axis=2)).astype(jnp.bfloat16)
        back_sum = back_sum.at[device_col, safe_rows].add(widen(back_rows))
        return ((mix_sum, back_sum), (gate_w_grad, up_w_grad, down_w_grad, gate_dot))
    carry_start = (jnp.zeros((N_DP, TOKENS_PER_SHARD, MODEL_DIMENSION), jnp.float32), jnp.zeros((N_DP, TOKENS_PER_SHARD, MODEL_DIMENSION), jnp.float32))
    (mix_sum, back_sum), (gate_experts_grad, up_experts_grad, down_experts_grad, gate_dots) = lax.scan(expert_step, carry_start, (jnp.arange(EXPERT_TOTAL, dtype=jnp.int32), gate_experts, up_experts, down_experts))
    block_output = (middle_all + mix_sum).astype(jnp.bfloat16).reshape(TOKENS, MODEL_DIMENSION)
    gate_slot_grad = jnp.transpose(gate_dots, (1, 0, 2)).reshape(N_DP, EXPERT_TOTAL * CAP)
    gate_grad_all = jnp.take_along_axis(gate_slot_grad, slot_index.reshape(N_DP, TOKENS_PER_SHARD * TOPK), axis=1).reshape(N_DP, TOKENS_PER_SHARD, TOPK)

    def backward_device(carry, device_inputs):
        x_rows, segment_row, grad_rows, ffn_back, gate_grad_row, choose_row, prob_row, select_row, gate_row = device_inputs
        piece_list = attention_pieces(x_rows, segment_row, attn_gain, query_weight, key_projection, value_projection, query_norm_gain, key_norm_gain, output_projection)
        ffn_in = (piece_list['normed_two'] * ffn_gain).astype(jnp.bfloat16)
        select_total = lax.optimization_barrier(jnp.sum(select_row, axis=-1, keepdims=True))
        select_grad = (gate_grad_row - lax.optimization_barrier(jnp.sum(gate_grad_row * gate_row, axis=-1, keepdims=True))) / select_total
        prob_grad = lax.optimization_barrier(jnp.sum(choose_row * select_grad[:, :, None], axis=1))
        logit_grad = (prob_row * (prob_grad - lax.optimization_barrier(jnp.sum(prob_grad * prob_row, axis=-1, keepdims=True)))).astype(jnp.bfloat16)
        router_part = jnp.dot(ffn_in.T, logit_grad, preferred_element_type=jnp.float32)
        ffn_grad = ffn_back + jnp.dot(logit_grad, router_weight.T, preferred_element_type=jnp.float32)
        normed_two = piece_list['normed_two']
        ffn_gain_part = lax.optimization_barrier(jnp.sum(ffn_grad * normed_two, axis=0))
        mid_grad = grad_rows.astype(jnp.float32) + norm_reverse(ffn_grad * ffn_gain, normed_two, piece_list['scale_two'])
        middle_gradient_second = mid_grad.astype(jnp.bfloat16)
        out_w_part = jnp.dot(middle_gradient_second.T, piece_list['attn_flat'], preferred_element_type=jnp.float32)
        attention_output_gradient = jnp.dot(middle_gradient_second, output_projection, preferred_element_type=jnp.float32).astype(jnp.bfloat16).reshape(TOKENS_PER_SHARD, KEY_VALUE_HEADS, group_width, HEAD_SIZE)
        attn_out = piece_list['attn_out']
        prob_full = jnp.exp(piece_list['scores'] - piece_list['log_sums'])
        prob_half = prob_full.astype(jnp.bfloat16)
        row_delta = lax.optimization_barrier(jnp.sum(widen(attention_output_gradient) * widen(attn_out), axis=-1))
        row_delta = jnp.transpose(row_delta, (1, 2, 0))[..., None]
        value_gradient = jnp.einsum('kgqs,qkgd->skd', widen(prob_half), widen(attention_output_gradient))
        prob_grad_attn = jnp.einsum('qkgd,skd->kgqs', widen(attention_output_gradient), widen(piece_list['value_rows']))
        score_grad = (prob_full * (prob_grad_attn - row_delta) * HEAD_SIZE ** (-0.5)).astype(jnp.bfloat16)
        query_grad = jnp.einsum('kgqs,skd->qkgd', widen(score_grad), widen(piece_list['key_rot'])).reshape(TOKENS_PER_SHARD, QUERY_HEADS, HEAD_SIZE)
        key_grad = jnp.einsum('kgqs,qkgd->skd', widen(score_grad), widen(piece_list['query_rot']))
        cosine_table = piece_list['cosine']
        sine_lookup = piece_list['sine_table']
        query_back = rotate_back(query_grad, cosine_table, sine_lookup)
        query_gain_part = lax.optimization_barrier(jnp.sum(query_back * piece_list['query_hat'], axis=(0, 1)))
        query_raw_grad = norm_reverse(query_back * query_norm_gain, piece_list['query_hat'], piece_list['query_scale']).astype(jnp.bfloat16).reshape(TOKENS_PER_SHARD, QUERY_HEADS * HEAD_SIZE)
        key_reverse = rotate_back(key_grad, cosine_table, sine_lookup)
        key_gain_part = lax.optimization_barrier(jnp.sum(key_reverse * piece_list['key_hat'], axis=(0, 1)))
        key_unnormed_gradient = norm_reverse(key_reverse * key_norm_gain, piece_list['key_hat'], piece_list['key_scale']).astype(jnp.bfloat16).reshape(TOKENS_PER_SHARD, KEY_VALUE_HEADS * HEAD_SIZE)
        value_gradient_second = value_gradient.astype(jnp.bfloat16).reshape(TOKENS_PER_SHARD, KEY_VALUE_HEADS * HEAD_SIZE)
        attention_input = piece_list['attn_in']
        query_w_part = jnp.dot(attention_input.T, query_raw_grad, preferred_element_type=jnp.float32)
        key_w_part = jnp.dot(attention_input.T, key_unnormed_gradient, preferred_element_type=jnp.float32)
        value_w_part = jnp.dot(attention_input.T, value_gradient_second, preferred_element_type=jnp.float32)
        attn_in_grad = jnp.dot(query_raw_grad, query_weight.T, preferred_element_type=jnp.float32) + jnp.dot(key_unnormed_gradient, key_projection.T, preferred_element_type=jnp.float32) + jnp.dot(value_gradient_second, value_projection.T, preferred_element_type=jnp.float32)
        normed_one = piece_list['normed_one']
        attn_gain_part = lax.optimization_barrier(jnp.sum(attn_in_grad * normed_one, axis=0))
        input_rows = (mid_grad + norm_reverse(attn_in_grad * attn_gain, normed_one, piece_list['scale_one'])).astype(jnp.bfloat16)
        terms = (query_w_part, key_w_part, value_w_part, out_w_part, router_part, attn_gain_part, ffn_gain_part, query_gain_part, key_gain_part)
        new_carry = tuple((total + term for total, term in zip(carry, terms)))
        return (new_carry, input_rows)
    zeroed_gradients = (jnp.zeros((MODEL_DIMENSION, QUERY_HEADS * HEAD_SIZE), jnp.float32), jnp.zeros((MODEL_DIMENSION, KEY_VALUE_HEADS * HEAD_SIZE), jnp.float32), jnp.zeros((MODEL_DIMENSION, KEY_VALUE_HEADS * HEAD_SIZE), jnp.float32), jnp.zeros((MODEL_DIMENSION, QUERY_HEADS * HEAD_SIZE), jnp.float32), jnp.zeros((MODEL_DIMENSION, EXPERT_TOTAL), jnp.float32), jnp.zeros((MODEL_DIMENSION,), jnp.float32), jnp.zeros((MODEL_DIMENSION,), jnp.float32), jnp.zeros((HEAD_SIZE,), jnp.float32), jnp.zeros((HEAD_SIZE,), jnp.float32))
    sums, input_grad = lax.scan(backward_device, zeroed_gradients, (input_dev, segment_ids, grad_dev, back_sum, gate_grad_all, choose_float, router_prob, selected, gate_values))
    query_weight_grad, key_weight_grad, value_weight_grad, out_weight_grad, router_weight_grad, attn_gain_grad, ffn_gain_grad, query_gain_grad, key_gain_grad = sums
    return (block_output, input_grad.reshape(TOKENS, MODEL_DIMENSION), attn_gain_grad, query_weight_grad, key_weight_grad, value_weight_grad, query_gain_grad, key_gain_grad, out_weight_grad, ffn_gain_grad, router_weight_grad, gate_experts_grad, up_experts_grad, down_experts_grad)
```

```python
import jax
import jax.numpy as jnp
from jax import lax
from jax.sharding import PartitionSpec as P

EPS = 1e-06
THETA = 1000000.0
F32 = jnp.float32
BF16 = jnp.bfloat16


def rms_scale(values):
    return lax.rsqrt(jnp.mean(values * values, axis=-1, keepdims=True) + EPS)


def norm_reverse(grad_rows, normed, scale_rows):
    return scale_rows * (grad_rows - normed * jnp.mean(grad_rows * normed, axis=-1, keepdims=True))


def dot_nn(a, b):
    return lax.dot_general(a, b, (((1,), (0,)), ((), ())), preferred_element_type=F32)


def dot_nt(a, b):
    return lax.dot_general(a, b, (((1,), (1,)), ((), ())), preferred_element_type=F32)


def dot_tn(a, b):
    return lax.dot_general(a, b, (((0,), (0,)), ((), ())), preferred_element_type=F32)


def swap(value, bit, count):
    return lax.ppermute(value, "dp", [(i, i ^ bit) for i in range(count)])


def shift(value, step, count):
    return lax.ppermute(value, "tensor", [(i, (i + step) % count) for i in range(count)])


def gather_dp(shard, count):
    if count == 8:
        half = shard.shape[0] // 2
        along_x = swap(shard, 2, count)
        along_y = swap(shard, 4, count)
        mate = swap(shard, 1, count)
        diag_lo = swap(along_y[:half], 2, count)
        diag_hi = swap(along_x[half:], 4, count)
        mate_x = swap(along_x, 1, count)
        mate_y = swap(along_y, 1, count)
        diag = jnp.concatenate([diag_lo, diag_hi], 0)
        mate_d = swap(diag, 1, count)
        return [shard, mate, along_x, mate_x, along_y, mate_y, diag, mate_d]
    return [lax.all_gather(shard, "dp", axis=0, tiled=True)]


def add_b(a, b):
    return (a.astype(F32) + b.astype(F32)).astype(BF16)


def scatter_dp(rows, count):
    if count == 8:
        size = rows.shape[0] // count
        half = size // 2
        chunks = [rows[r * size : (r + 1) * size] for r in range(count)]
        pair = {}
        for r in (6, 4, 2, 0):
            pair[r] = add_b(chunks[r], swap(chunks[r + 1], 1, count))
        from_x = swap(pair[6][:half], 2, count)
        from_y = swap(pair[6][half:], 4, count)
        to_y = jnp.concatenate([add_b(pair[4][:half], from_x), pair[4][half:]], 0)
        to_x = jnp.concatenate([pair[2][:half], add_b(pair[2][half:], from_y)], 0)
        got_x = swap(to_x, 2, count)
        got_y = swap(to_y, 4, count)
        return (pair[0].astype(F32) + got_x.astype(F32) + got_y.astype(F32)).astype(BF16)
    return lax.psum_scatter(rows, "dp", scatter_dimension=0, tiled=True)


def gather_z(shard, count):
    if count == 4:
        half = shard.shape[1] // 2
        prev = shift(shard, 1, count)
        after = shift(shard, -1, count)
        far_lo = shift(prev[:, :half], 1, count)
        far_hi = shift(after[:, half:], -1, count)
        far = jnp.concatenate([far_lo, far_hi], 1)
        return jnp.concatenate([shard, after, far, prev], 0)
    return jnp.concatenate([shard] + [shift(shard, -r, count) for r in range(1, count)], 0)


def scatter_z(rows, count):
    size = rows.shape[0] // count
    block = [rows[r * size : (r + 1) * size] for r in range(count)]
    if count == 4:
        half = rows.shape[1] // 2
        lo = shift(block[2][:, :half], 1, count)
        hi = shift(block[2][:, half:], -1, count)
        up = jnp.concatenate([add_b(block[1][:, :half], lo), block[1][:, half:]], 1)
        down = jnp.concatenate([block[3][:, :half], add_b(block[3][:, half:], hi)], 1)
        got_up = shift(up, 1, count)
        got_down = shift(down, -1, count)
        return block[0].astype(F32) + got_up.astype(F32) + got_down.astype(F32)
    total = block[0].astype(F32)
    for r in range(1, count):
        total = total + shift(block[r], r, count).astype(F32)
    return total


def roll_rows(rows, amount):
    return jnp.roll(rows, amount, axis=0)


def rope_apply(values, cos_rows, sin_rows):
    half = values.shape[-1] // 2
    low, high = values[..., :half], values[..., half:]
    c, s = cos_rows[:, None, :], sin_rows[:, None, :]
    return jnp.concatenate([low * c - high * s, high * c + low * s], axis=-1)


def rope_back(values, cos_rows, sin_rows):
    half = values.shape[-1] // 2
    low, high = values[..., :half], values[..., half:]
    c, s = cos_rows[:, None, :], sin_rows[:, None, :]
    return jnp.concatenate([low * c + high * s, high * c - low * s], axis=-1)


def local(
    block_input,
    segment_ids,
    expert_ids,
    attn_gain,
    query_weight,
    key_projection,
    value_projection,
    query_norm_gain,
    key_norm_gain,
    output_projection,
    ffn_gain,
    router_weight,
    gate_experts,
    up_experts,
    down_experts,
    out_grad,
):
    tokens, width = block_input.shape
    head_dim = query_norm_gain.shape[0]
    experts_dev, _, hidden_dev = gate_experts.shape
    n_dp = lax.axis_size("dp")
    n_t = lax.axis_size("tensor")
    num_experts = experts_dev * n_dp
    part = tokens // n_t
    flat = experts_dev * hidden_dev
    t_index = lax.axis_index("tensor")
    d_index = lax.axis_index("dp")
    turn = t_index * part
    scale_value = head_dim ** (-0.5)

    x_rows = roll_rows(block_input, -turn)
    seg = roll_rows(segment_ids[0], -turn)
    ids = roll_rows(expert_ids, -turn)
    dy_rows = roll_rows(out_grad, -turn)
    order = (jnp.arange(tokens, dtype=jnp.int32) + turn) % tokens

    dy_chunks = gather_dp(dy_rows, n_dp)
    ids_all = jnp.concatenate(gather_dp(ids, n_dp), 0)
    dy_all = jnp.concatenate(dy_chunks, 0)

    inputs_f = x_rows.astype(F32)
    scale_one = rms_scale(inputs_f)
    normed_one = inputs_f * scale_one
    attn_in = (normed_one * attn_gain).astype(BF16)

    same = seg[:, None] == seg[None, :]
    earlier = order[None, :] < order[:, None]
    positions = jnp.sum((same & earlier).astype(jnp.int32), axis=1)
    half_dim = head_dim // 2
    frequency = THETA ** (-(jnp.arange(half_dim, dtype=F32) * 2.0) / head_dim)
    angles = positions.astype(F32)[:, None] * frequency[None, :]
    cos_rows, sin_rows = jnp.cos(angles), jnp.sin(angles)
    allowed = same & (order[None, :] <= order[:, None])

    q_raw = dot_nn(attn_in, query_weight).reshape(tokens, -1, head_dim)
    q_scale = rms_scale(q_raw)
    q_hat = q_raw * q_scale
    k_raw = dot_nn(attn_in, key_projection).reshape(tokens, -1, head_dim)
    k_scale = rms_scale(k_raw)
    k_hat = k_raw * k_scale
    k_rot = rope_apply(k_hat * key_norm_gain, cos_rows, sin_rows).astype(BF16)
    v_rows = dot_nn(attn_in, value_projection).astype(BF16).reshape(tokens, -1, head_dim)
    heads = q_raw.shape[1]
    kv = k_raw.shape[1]
    group = heads // kv
    q_rot = rope_apply(q_hat * query_norm_gain, cos_rows, sin_rows).astype(BF16)
    q_rot = q_rot.reshape(tokens, kv, group, head_dim)
    scores = jnp.einsum("qkgd,skd->kgqs", q_rot, k_rot, preferred_element_type=F32) * scale_value
    scores = jnp.where(allowed, scores, -jnp.inf)
    top = jnp.max(scores, axis=-1, keepdims=True)
    weights = jnp.exp(scores - top)
    totals = jnp.sum(weights, axis=-1, keepdims=True)
    probs = weights / totals
    probs_b = probs.astype(BF16)
    attn_out = jnp.einsum("kgqs,skd->qkgd", probs_b, v_rows, preferred_element_type=F32)
    attn_out = attn_out.astype(BF16)
    attn_flat = attn_out.reshape(tokens, heads * head_dim)
    attn_part = dot_nt(attn_flat, output_projection).astype(BF16)
    attn_sum = scatter_z(attn_part, n_t)

    x_own = inputs_f[:part]
    ids_own = ids[:part]
    middle = x_own + attn_sum
    scale_two = rms_scale(middle)
    normed_two = middle * scale_two
    ffn_own = (normed_two * ffn_gain).astype(BF16)
    ffn_rows = gather_z(ffn_own, n_t)
    x_all = jnp.concatenate(gather_dp(ffn_rows, n_dp), 0)

    def router(rows, chosen):
        logits = dot_nn(rows, router_weight)
        raised = jnp.exp(logits - jnp.max(logits, axis=-1, keepdims=True))
        prob = raised / jnp.sum(raised, axis=-1, keepdims=True)
        names = jnp.arange(num_experts, dtype=jnp.int32)
        mask = jnp.any(chosen[:, :, None] == names[None, None, :], axis=1).astype(F32)
        total = jnp.sum(prob * mask, axis=-1, keepdims=True)
        return prob, mask, total, prob * mask / total

    prob_own, mask_own, total_own, gate_own = router(ffn_own, ids_own)
    gate_all = router(x_all, ids_all)[3]

    owner = d_index * experts_dev + jnp.arange(flat, dtype=jnp.int32) // hidden_dev
    names = jnp.arange(num_experts, dtype=jnp.int32)
    place = (names[:, None] == owner[None, :]).astype(F32)
    gate_wide = jnp.dot(gate_all, place, precision=lax.Precision.HIGHEST)

    wg = jnp.transpose(gate_experts, (0, 2, 1)).reshape(flat, width)
    wu = jnp.transpose(up_experts, (0, 2, 1)).reshape(flat, width)
    wd = down_experts.reshape(flat, width)

    d_hidden = dot_nt(dy_all, wd)
    gate_pre = dot_nt(x_all, wg)
    up_pre = dot_nt(x_all, wu)
    sig = jax.nn.sigmoid(gate_pre)
    act = gate_pre * sig
    hidden = act * up_pre
    hidden_g = (hidden * gate_wide).astype(BF16)
    gate_grads = lax.dot_general(
        hidden * d_hidden, place, (((1,), (1,)), ((), ())), precision=lax.Precision.HIGHEST
    )
    hidden_grad = d_hidden * gate_wide
    dg = (hidden_grad * up_pre * sig * (1.0 + gate_pre * (1.0 - sig))).astype(BF16)
    du = (hidden_grad * act).astype(BF16)
    back = (dot_nn(dg, wg) + dot_nn(du, wu)).astype(BF16)
    pad = (-num_experts) % 128
    back = jnp.concatenate([back, jnp.pad(gate_grads, ((0, 0), (0, pad))).astype(BF16)], 1)
    back_sum = scatter_dp(back, n_dp)
    back_own = scatter_z(back_sum, n_t)
    ffn_back = back_own[:, :width]
    gate_grad = back_own[:, width : width + num_experts]

    mix = dot_nn(hidden_g, wd).astype(BF16)
    mix_sum = scatter_dp(mix, n_dp)
    mix_own = scatter_z(mix_sum, n_t)
    block_out = gather_z((middle + mix_own).astype(BF16), n_t)
    block_output = roll_rows(block_out, turn)

    down_grad = dot_tn(hidden_g, dy_all).reshape(experts_dev, hidden_dev, width)
    gate_w_grad = dot_tn(dg, x_all).reshape(experts_dev, hidden_dev, width).transpose(0, 2, 1)
    up_w_grad = dot_tn(du, x_all).reshape(experts_dev, hidden_dev, width).transpose(0, 2, 1)

    select_grad = (gate_grad - jnp.sum(gate_grad * gate_own, axis=-1, keepdims=True)) / total_own
    prob_grad = mask_own * select_grad
    logit_grad = (
        prob_own * (prob_grad - jnp.sum(prob_grad * prob_own, axis=-1, keepdims=True))
    ).astype(BF16)
    router_part = dot_tn(ffn_own, logit_grad)
    ffn_grad = ffn_back + dot_nt(logit_grad, router_weight)
    ffn_gain_part = jnp.sum(ffn_grad * normed_two, axis=0)
    mid_grad = dy_rows[:part].astype(F32) + norm_reverse(ffn_grad * ffn_gain, normed_two, scale_two)
    mid_rows = gather_z(mid_grad.astype(BF16), n_t)

    d_attn = dot_nn(mid_rows, output_projection).astype(BF16)
    d_out = d_attn.reshape(tokens, kv, group, head_dim)
    delta = jnp.sum(d_out.astype(F32) * attn_out.astype(F32), axis=-1)
    delta = jnp.transpose(delta, (1, 2, 0))[..., None]
    v_grad = jnp.einsum("kgqs,qkgd->skd", probs_b, d_out, preferred_element_type=F32)
    p_grad = jnp.einsum("qkgd,skd->kgqs", d_out, v_rows, preferred_element_type=F32)
    s_grad = (probs * (p_grad - delta) * scale_value).astype(BF16)
    q_grad = jnp.einsum("kgqs,skd->qkgd", s_grad, k_rot, preferred_element_type=F32)
    k_grad = jnp.einsum("kgqs,qkgd->skd", s_grad, q_rot, preferred_element_type=F32)
    q_back = rope_back(q_grad.reshape(tokens, heads, head_dim), cos_rows, sin_rows)
    q_gain_part = jnp.sum(q_back * q_hat, axis=(0, 1))
    q_raw_grad = norm_reverse(q_back * query_norm_gain, q_hat, q_scale).astype(BF16)
    q_raw_grad = q_raw_grad.reshape(tokens, -1)
    k_back = rope_back(k_grad, cos_rows, sin_rows)
    k_gain_part = jnp.sum(k_back * k_hat, axis=(0, 1))
    k_raw_grad = norm_reverse(k_back * key_norm_gain, k_hat, k_scale).astype(BF16)
    k_raw_grad = k_raw_grad.reshape(tokens, -1)
    v_grad_b = v_grad.astype(BF16).reshape(tokens, -1)

    in_part = (
        dot_nt(q_raw_grad, query_weight)
        + dot_nt(k_raw_grad, key_projection)
        + dot_nt(v_grad_b, value_projection)
    ).astype(BF16)
    attn_in_grad = scatter_z(in_part, n_t)
    normed_own = normed_one[:part]
    attn_gain_part = jnp.sum(attn_in_grad * normed_own, axis=0)
    input_own = mid_grad + norm_reverse(attn_in_grad * attn_gain, normed_own, scale_one[:part])
    input_grad = roll_rows(gather_z(input_own.astype(BF16), n_t), turn)

    def weight_grad(rows_dp, columns_dp):
        return dot_tn(jnp.concatenate(rows_dp, 0), jnp.concatenate(columns_dp, 0))

    slab = width // n_dp

    def spread(rows):
        if n_dp != 8:
            return [lax.all_to_all(rows, "dp", split_axis=1, concat_axis=0, tiled=True)]
        out = []
        for r in range(n_dp):
            piece = lax.dynamic_slice_in_dim(rows, (d_index ^ r) * slab, slab, 1)
            out.append(piece if r == 0 else swap(piece, r, n_dp))
        return out

    attn_in_slab = spread(attn_in)
    mid_slab = spread(mid_rows)
    out_weight_grad = weight_grad(mid_slab, gather_dp(attn_flat, n_dp))
    qkv_grad = jnp.concatenate([q_raw_grad, k_raw_grad, v_grad_b], 1)
    qkv_w = weight_grad(attn_in_slab, gather_dp(qkv_grad, n_dp))
    q_cols = heads * head_dim
    kv_cols = kv * head_dim
    query_weight_grad = qkv_w[:, :q_cols]
    key_weight_grad = qkv_w[:, q_cols : q_cols + kv_cols]
    value_weight_grad = qkv_w[:, q_cols + kv_cols :]

    router_sum = lax.psum(
        lax.psum_scatter(router_part.astype(BF16), "dp", scatter_dimension=0, tiled=True), "tensor"
    ).astype(F32)
    gains = jnp.concatenate([attn_gain_part, ffn_gain_part, q_gain_part, k_gain_part])
    gains = lax.psum(gains, ("dp", "tensor"))

    def mine(vector):
        size = vector.shape[0] // n_dp
        return lax.dynamic_slice_in_dim(vector, d_index * size, size, 0)

    return (
        block_output,
        input_grad,
        mine(gains[:width]),
        query_weight_grad,
        key_weight_grad,
        value_weight_grad,
        mine(gains[2 * width : 2 * width + head_dim]),
        mine(gains[2 * width + head_dim :]),
        out_weight_grad,
        mine(gains[width : 2 * width]),
        router_sum,
        gate_w_grad,
        up_w_grad,
        down_grad,
    )


def solution(mesh):
    return jax.shard_map(
        local,
        mesh=mesh,
        in_specs=(
            P("dp", None),
            P("dp", None),
            P("dp", None),
            P(),
            P(None, "tensor"),
            P(None, "tensor"),
            P(None, "tensor"),
            P(),
            P(),
            P(None, "tensor"),
            P(),
            P(),
            P("dp", None, "tensor"),
            P("dp", None, "tensor"),
            P("dp", "tensor", None),
            P("dp", None),
        ),
        out_specs=(
            P("dp", None),
            P("dp", None),
            P("dp"),
            P("dp", "tensor"),
            P("dp", "tensor"),
            P("dp", "tensor"),
            P("dp"),
            P("dp"),
            P("dp", "tensor"),
            P("dp"),
            P("dp", None),
            P("dp", None, "tensor"),
            P("dp", None, "tensor"),
            P("dp", "tensor", None),
        ),
        check_vma=False,
    )
```

```python
import functools

import jax
import jax.numpy as jnp
from jax import lax
from jax.experimental import pallas as pl
from jax.experimental.pallas import tpu as pltpu
from jax.sharding import PartitionSpec as P

EPS = 1e-06
THETA = 1000000.0
F32 = jnp.float32
BF16 = jnp.bfloat16
LANES = 128


def rms_scale(values):
    return lax.rsqrt(jnp.mean(values * values, axis=-1, keepdims=True) + EPS)


def norm_reverse(grad_rows, normed, scale_rows):
    return scale_rows * (grad_rows - normed * jnp.mean(grad_rows * normed, axis=-1, keepdims=True))


def dot_nn(a, b):
    return lax.dot_general(a, b, (((1,), (0,)), ((), ())), preferred_element_type=F32)


def dot_nt(a, b):
    return lax.dot_general(a, b, (((1,), (1,)), ((), ())), preferred_element_type=F32)


def dot_tn(a, b):
    return lax.dot_general(a, b, (((0,), (0,)), ((), ())), preferred_element_type=F32)


def swap(value, bit, count):
    return lax.ppermute(value, "dp", [(i, i ^ bit) for i in range(count)])


def shift(value, step, count):
    return lax.ppermute(value, "tensor", [(i, (i + step) % count) for i in range(count)])


def after(value, *first):
    return lax.optimization_barrier((value,) + first)[0]


def add_b(a, b):
    return (a.astype(F32) + b.astype(F32)).astype(BF16)


def gather_eight(shard):
    half = shard.shape[0] // 16 * 8
    along_x = swap(shard, 2, 8)
    along_y = swap(shard, 4, 8)
    mate = swap(shard, 1, 8)
    diag_lo = swap(along_y[:half], 2, 8)
    diag_hi = swap(along_x[half:], 4, 8)
    mate_x = swap(along_x, 1, 8)
    mate_y = swap(along_y, 1, 8)
    diag = jnp.concatenate([diag_lo, diag_hi], 0)
    mate_d = swap(diag, 1, 8)
    return [shard, mate, along_x, mate_x, along_y, mate_y, diag, mate_d]


def scatter_eight(chunks, *first):
    mates = {r: swap(chunks[r + 1], 1, 8) for r in (0, 2, 4, 6)}
    sent = {r: swap(add_b(chunks[r], mates[r]), r, 8) for r in (2, 4, 6)}
    sent = after(sent, *first)
    total = chunks[0].astype(F32) + mates[0].astype(F32)
    for r in (2, 4, 6):
        total = total + sent[r].astype(F32)
    return total.astype(BF16)


def row_block(rows, index, count):
    size = rows.shape[0] // count
    return lax.dynamic_slice_in_dim(rows, (index % count) * size, size, 0)


def scatter_z(rows, index, count):
    if count != 4:
        return lax.psum_scatter(rows, "tensor", scatter_dimension=0, tiled=True).astype(F32)
    half = rows.shape[1] // 2
    far = row_block(rows, index + 2, count)
    lo = shift(far[:, :half], 1, count)
    hi = shift(far[:, half:], -1, count)
    zero = jnp.zeros_like(lo)
    up = add_b(row_block(rows, index + 1, count), jnp.concatenate([lo, zero], 1))
    down = add_b(row_block(rows, index + 3, count), jnp.concatenate([zero, hi], 1))
    got_up = shift(up, 1, count)
    got_down = shift(down, -1, count)
    own = row_block(rows, index, count).astype(F32)
    return own + got_up.astype(F32) + got_down.astype(F32)


def join_kernel(place, own, nxt, prev, far_lo, far_hi, out):
    size, width = own.shape
    half = width // 2
    t = place[0]

    def rows(step):
        return pl.ds(pl.multiple_of(lax.rem(t + step, 4) * size, size), size)

    out[rows(0), :] = own[...]
    out[rows(1), :] = nxt[...]
    out[rows(2), :half] = far_lo[...]
    out[rows(2), half:] = far_hi[...]
    out[rows(3), :] = prev[...]


def gather_z(shard, index, count):
    if count != 4:
        return lax.all_gather(shard, "tensor", axis=0, tiled=True)
    size, width = shard.shape
    half = width // 2
    prev = shift(shard, 1, count)
    nxt = shift(shard, -1, count)
    far_lo = shift(prev[:, :half], 1, count)
    far_hi = shift(nxt[:, half:], -1, count)
    vmem = pl.BlockSpec(memory_space=pltpu.VMEM)
    return pl.pallas_call(
        join_kernel,
        in_specs=[pl.BlockSpec(memory_space=pltpu.SMEM)] + [vmem] * 5,
        out_specs=vmem,
        out_shape=jax.ShapeDtypeStruct((count * size, width), shard.dtype),
        name="join_rows",
    )(index.reshape(1), shard, nxt, prev, far_lo, far_hi)


def split_dot(a, b, form):
    high = a.astype(BF16)
    low = (a - high.astype(F32)).astype(BF16)
    return form(high, b) + form(low, b)


def stage_kernel(count, xa, xb, dh_ref, ma, mb, wr, wg, wu, place, back_a, back_b, hg, dg, du):
    rows, width = xa.shape
    x = jnp.concatenate([xa[...], xb[...]], 0)
    logits = dot_nt(x, wr[...])
    lane = lax.broadcasted_iota(jnp.int32, logits.shape, 1)
    logits = jnp.where(lane < count, logits, -1e30)
    raised = jnp.exp(logits - jnp.max(logits, axis=-1, keepdims=True))
    chosen = raised * jnp.concatenate([ma[...], mb[...]], 0).astype(F32)
    gate = chosen / jnp.sum(chosen, axis=-1, keepdims=True)
    wide = split_dot(gate, place[...], dot_nn)
    g = dot_nt(x, wg[...])
    u = dot_nt(x, wu[...])
    dh = dh_ref[...].astype(F32)
    sig = jax.nn.sigmoid(g)
    act = g * sig
    hidden = act * u
    hg[...] = (hidden * wide).astype(BF16)
    grads = split_dot(hidden * dh, place[...], dot_nt)
    scaled = dh * wide
    dg_b = (scaled * u * sig * (1.0 + g * (1.0 - sig))).astype(BF16)
    du_b = (scaled * act).astype(BF16)
    dg[...] = dg_b
    du[...] = du_b
    back = (dot_nn(dg_b, wg[...]) + dot_nn(du_b, wu[...])).astype(BF16)
    back_a[:, :width] = back[:rows]
    back_b[:, :width] = back[rows:]
    back_a[:, width:] = grads[:rows].astype(BF16)
    back_b[:, width:] = grads[rows:].astype(BF16)


def expert_stage(xa, xb, dh, ma, mb, wr, wg, wu, place, count):
    rows, width = xa.shape
    flat = wg.shape[0]
    wide = jax.ShapeDtypeStruct((rows, width + LANES), BF16)
    tall = jax.ShapeDtypeStruct((2 * rows, flat), BF16)
    whole = lambda a: pl.BlockSpec(a.shape, lambda i: (0, 0))
    mask = pl.BlockSpec((rows, LANES), lambda i: (0, width // LANES))
    return pl.pallas_call(
        functools.partial(stage_kernel, count),
        grid=(1,),
        in_specs=[whole(xa), whole(xb), whole(dh), mask, mask, whole(wr), whole(wg), whole(wu), whole(place)],
        out_specs=[whole(a) for a in (wide, wide, tall, tall, tall)],
        out_shape=[wide, wide, tall, tall, tall],
        cost_estimate=pl.CostEstimate(
            flops=16 * rows * flat * width,
            transcendentals=2 * rows * flat,
            bytes_accessed=4 * (4 * rows * width + 2 * flat * width),
        ),
        name="expert_stage",
    )(xa, xb, dh, ma, mb, wr, wg, wu, place)


def hidden_kernel(ya, yb, wd, dh):
    rows = ya.shape[0]
    width = wd.shape[1]
    dh[:rows] = dot_nt(ya[:, :width], wd[...]).astype(BF16)
    dh[rows:] = dot_nt(yb[:, :width], wd[...]).astype(BF16)


def hidden_back(ya, yb, wd):
    rows = ya.shape[0]
    flat, width = wd.shape
    vmem = pl.BlockSpec(memory_space=pltpu.VMEM)
    return pl.pallas_call(
        hidden_kernel,
        in_specs=[vmem] * 3,
        out_specs=vmem,
        out_shape=jax.ShapeDtypeStruct((2 * rows, flat), BF16),
        cost_estimate=pl.CostEstimate(
            flops=4 * rows * flat * width,
            transcendentals=0,
            bytes_accessed=4 * rows * width + 2 * flat * width,
        ),
        name="hidden_back",
    )(ya, yb, wd)


def mix_kernel(hg, wd, mix_a, mix_b):
    rows = mix_a.shape[0]
    mix = dot_nn(hg[...], wd[...]).astype(BF16)
    mix_a[...] = mix[:rows]
    mix_b[...] = mix[rows:]


def mix_rows(hg, wd):
    rows, flat = hg.shape
    width = wd.shape[1]
    half = jax.ShapeDtypeStruct((rows // 2, width), BF16)
    vmem = pl.BlockSpec(memory_space=pltpu.VMEM)
    return pl.pallas_call(
        mix_kernel,
        in_specs=[vmem] * 2,
        out_specs=[vmem] * 2,
        out_shape=[half, half],
        cost_estimate=pl.CostEstimate(
            flops=2 * rows * flat * width,
            transcendentals=0,
            bytes_accessed=2 * rows * width + 2 * flat * width,
        ),
        name="mix_rows",
    )(hg, wd)


def weight_kernel(n_rows, n_left, *refs):
    right = refs[:n_rows]
    left = refs[n_rows : n_rows + n_left]
    outs = refs[n_rows + n_left :]
    per = n_left // len(outs)
    rows = right[0].shape[0]
    for o, out in enumerate(outs):
        total = None
        for s in range(per):
            lhs = left[o * per + s]
            for h in range(2):
                term = dot_tn(lhs[h * rows : (h + 1) * rows, :], right[2 * s + h][...])
                total = term if total is None else total + term
        out[...] = total


def weight_grads(rows_list, left_lists, width):
    rows = rows_list[0].shape[0]
    flat = left_lists[0][0].shape[1]
    block = 512
    lefts = [a for group in left_lists for a in group]
    n = len(rows_list)
    return pl.pallas_call(
        functools.partial(weight_kernel, n, len(lefts)),
        grid=(width // block,),
        in_specs=[pl.BlockSpec((rows, block), lambda j: (0, j))] * n
        + [pl.BlockSpec(a.shape, lambda j: (0, 0)) for a in lefts],
        out_specs=[pl.BlockSpec((flat, block), lambda j: (0, j))] * len(left_lists),
        out_shape=[jax.ShapeDtypeStruct((flat, width), F32)] * len(left_lists),
        cost_estimate=pl.CostEstimate(
            flops=2 * n * rows * flat * width * len(left_lists),
            transcendentals=0,
            bytes_accessed=4 * flat * width * len(left_lists) + 2 * n * rows * width,
        ),
        name="weight_grads",
    )(*rows_list, *lefts)


def tail_kernel(q_cols, kv_cols, *refs):
    slabs, qkv, ffn, attn = refs[1:9], refs[9:17], refs[17:25], refs[25:33]
    q_out, k_out, v_out, o_out, r_out, gain_out = refs[33:]
    rows = ffn[0].shape[0]
    slab = slabs[0].shape[1] // 2
    main = router = out = gains = None
    for r in range(8):
        attn_in = slabs[r][:, :slab]
        mid = slabs[r][:, slab:]
        a = dot_tn(attn_in, qkv[r][:rows, : q_cols + 2 * kv_cols])
        b = dot_tn(ffn[r][...], qkv[r][:rows, q_cols + 2 * kv_cols :])
        c = dot_tn(mid, attn[r][...])
        d = qkv[r][rows:, :].astype(F32)
        main, router, out, gains = (
            (a, b, c, d) if r == 0 else (main + a, router + b, out + c, gains + d)
        )
    q_out[...] = main[:, :q_cols]
    k_out[...] = main[:, q_cols : q_cols + kv_cols]
    v_out[...] = main[:, q_cols + kv_cols :]
    o_out[...] = out
    r_out[...] = router
    gain_out[...] = gains


def tail_grads(d_index, slabs, qkv, ffn, attn_all, q_cols, kv_cols):
    slab = slabs[0].shape[1] // 2
    rows = ffn[0].shape[0]
    cols = qkv[0].shape[1]
    extra = qkv[0].shape[0] - rows
    whole = lambda shape: pl.BlockSpec(shape, lambda i, s: (0, 0))
    outs = [(slab, q_cols), (slab, kv_cols), (slab, kv_cols), (slab, q_cols), (slab, LANES)]
    outs.append((extra, cols))
    return pl.pallas_call(
        functools.partial(tail_kernel, q_cols, kv_cols),
        grid_spec=pltpu.PrefetchScalarGridSpec(
            num_scalar_prefetch=1,
            grid=(1,),
            in_specs=[whole(a.shape) for a in slabs]
            + [whole(a.shape) for a in qkv]
            + [pl.BlockSpec((rows, slab), lambda i, s: (0, s[0])) for _ in ffn]
            + [
                pl.BlockSpec((rows, q_cols), functools.partial(lambda r, i, s: (s[0] ^ r, 0), r))
                for r in range(8)
            ],
            out_specs=[whole(shape) for shape in outs],
        ),
        out_shape=[jax.ShapeDtypeStruct(shape, F32) for shape in outs],
        name="tail_grads",
    )(d_index.reshape(1), *slabs, *qkv, *ffn, *([attn_all] * 8))


def experts_eight(ffn_rows, hidden, masks, wr, wg, wu, place, count):
    x = gather_eight(ffn_rows)
    back, hg, dg, du = [], [], [], []
    for s in range(4):
        a, b, h, g, u = expert_stage(
            x[2 * s], x[2 * s + 1], hidden[s], masks[2 * s], masks[2 * s + 1], wr, wg, wu, place, count
        )
        back += [a, b]
        hg.append(h)
        dg.append(g)
        du.append(u)
    return x, back, hg, dg, du


def rope_apply(values, cos_rows, sin_rows):
    half = values.shape[-1] // 2
    low, high = values[..., :half], values[..., half:]
    c, s = cos_rows[:, None, :], sin_rows[:, None, :]
    return jnp.concatenate([low * c - high * s, high * c + low * s], axis=-1)


def rope_back(values, cos_rows, sin_rows):
    half = values.shape[-1] // 2
    low, high = values[..., :half], values[..., half:]
    c, s = cos_rows[:, None, :], sin_rows[:, None, :]
    return jnp.concatenate([low * c + high * s, high * c - low * s], axis=-1)


def local(
    block_input,
    segment_ids,
    expert_ids,
    attn_gain,
    query_weight,
    key_projection,
    value_projection,
    query_norm_gain,
    key_norm_gain,
    output_projection,
    ffn_gain,
    router_weight,
    gate_experts,
    up_experts,
    down_experts,
    out_grad,
):
    tokens, width = block_input.shape
    head_dim = query_norm_gain.shape[0]
    experts_dev, _, hidden_dev = gate_experts.shape
    n_dp = lax.axis_size("dp")
    n_t = lax.axis_size("tensor")
    num_experts = experts_dev * n_dp
    part = tokens // n_t
    flat = experts_dev * hidden_dev
    slab = width // n_dp
    t_index = lax.axis_index("tensor")
    d_index = lax.axis_index("dp")
    scale_value = head_dim ** (-0.5)
    eight = n_dp == 8
    names = jnp.arange(num_experts, dtype=jnp.int32)
    wg = jnp.transpose(gate_experts, (0, 2, 1)).reshape(flat, width)
    wu = jnp.transpose(up_experts, (0, 2, 1)).reshape(flat, width)
    wd = down_experts.reshape(flat, width)

    seg = segment_ids[0]
    order = jnp.arange(tokens, dtype=jnp.int32)
    inputs_f = block_input.astype(F32)
    scale_one = rms_scale(inputs_f)
    normed_one = inputs_f * scale_one
    attn_in = (normed_one * attn_gain).astype(BF16)
    same = seg[:, None] == seg[None, :]
    positions = jnp.sum((same & (order[None, :] < order[:, None])).astype(jnp.int32), axis=1)
    frequency = THETA ** (-(jnp.arange(head_dim // 2, dtype=F32) * 2.0) / head_dim)
    angles = positions.astype(F32)[:, None] * frequency[None, :]
    cos_rows, sin_rows = jnp.cos(angles), jnp.sin(angles)
    allowed = same & (order[None, :] <= order[:, None])
    q_raw = dot_nn(attn_in, query_weight).reshape(tokens, -1, head_dim)
    q_scale = rms_scale(q_raw)
    q_hat = q_raw * q_scale
    k_raw = dot_nn(attn_in, key_projection).reshape(tokens, -1, head_dim)
    k_scale = rms_scale(k_raw)
    k_hat = k_raw * k_scale
    k_rot = rope_apply(k_hat * key_norm_gain, cos_rows, sin_rows).astype(BF16)
    v_rows = dot_nn(attn_in, value_projection).astype(BF16).reshape(tokens, -1, head_dim)
    heads = q_raw.shape[1]
    kv = k_raw.shape[1]
    group = heads // kv
    q_cols = heads * head_dim
    kv_cols = kv * head_dim
    q_rot = rope_apply(q_hat * query_norm_gain, cos_rows, sin_rows).astype(BF16)
    q_rot = q_rot.reshape(tokens, kv, group, head_dim)
    scores = jnp.einsum("qkgd,skd->kgqs", q_rot, k_rot, preferred_element_type=F32) * scale_value
    scores = jnp.where(allowed, scores, -jnp.inf)
    top = jnp.max(scores, axis=-1, keepdims=True)
    weights = jnp.exp(scores - top)
    totals = jnp.sum(weights, axis=-1, keepdims=True)
    probs = weights / totals
    probs_b = probs.astype(BF16)
    attn_out = jnp.einsum("kgqs,skd->qkgd", probs_b, v_rows, preferred_element_type=F32)
    attn_out = attn_out.astype(BF16)
    attn_flat = attn_out.reshape(tokens, q_cols)
    attn_part = dot_nt(attn_flat, output_projection).astype(BF16)
    attn_sum = lax.psum(attn_part, "tensor").astype(F32)

    pad = -num_experts % LANES
    mask_own = jnp.any(expert_ids[:, :, None] == names[None, None, :], axis=1).astype(F32)
    owner = d_index * experts_dev + jnp.arange(flat, dtype=jnp.int32) // hidden_dev
    place = (names[:, None] == owner[None, :]).astype(BF16)
    place = jnp.pad(place, ((0, pad), (0, 0)))
    wr = jnp.pad(router_weight.T, ((0, pad), (0, 0)))
    dy_wide = jnp.concatenate([out_grad, jnp.pad(mask_own, ((0, 0), (0, pad))).astype(BF16)], 1)
    dy_wide = after(dy_wide, attn_part)
    if eight:
        dy_chunks = gather_eight(dy_wide)
        hidden = [hidden_back(dy_chunks[2 * s], dy_chunks[2 * s + 1], wd) for s in range(4)]
        attn_sum = after(attn_sum, dy_chunks[6], hidden[:3], place, wr)
    else:
        dy_all = lax.all_gather(dy_wide, "dp", axis=0, tiled=True)
        mask_all = dy_all[:, width : width + num_experts].astype(F32)
        dy_all = dy_all[:, :width]

    middle = inputs_f + attn_sum
    scale_two = rms_scale(middle)
    normed_two = middle * scale_two
    ffn_rows = (normed_two * ffn_gain).astype(BF16)
    logits = dot_nn(ffn_rows, router_weight)
    raised = jnp.exp(logits - jnp.max(logits, axis=-1, keepdims=True))
    prob = raised / jnp.sum(raised, axis=-1, keepdims=True)
    selected = prob * mask_own
    total_own = jnp.sum(selected, axis=-1, keepdims=True)
    gate_own = selected / total_own

    if eight:
        x_chunks, back, hg, dg, du = experts_eight(
            ffn_rows, hidden, dy_chunks, wr, wg, wu, place, num_experts
        )
        mix = [m for s in range(4) for m in mix_rows(hg[s], wd)]
        back_sum = scatter_eight(back, mix)
    else:
        x_all = lax.all_gather(ffn_rows, "dp", axis=0, tiled=True)
        lg = dot_nt(x_all, wr)[:, :num_experts]
        chosen = jnp.exp(lg - jnp.max(lg, axis=-1, keepdims=True)) * mask_all
        gate_all = chosen / jnp.sum(chosen, axis=-1, keepdims=True)
        spots = place[:num_experts].astype(F32)
        wide = jnp.dot(gate_all, spots, precision=lax.Precision.HIGHEST)
        d_hidden = dot_nt(dy_all, wd)
        gate_pre = dot_nt(x_all, wg)
        up_pre = dot_nt(x_all, wu)
        sig = jax.nn.sigmoid(gate_pre)
        act = gate_pre * sig
        hidden = act * up_pre
        hg_all = (hidden * wide).astype(BF16)
        grads = jnp.dot(hidden * d_hidden, spots.T, precision=lax.Precision.HIGHEST)
        scaled = d_hidden * wide
        dg_all = (scaled * up_pre * sig * (1.0 + gate_pre * (1.0 - sig))).astype(BF16)
        du_all = (scaled * act).astype(BF16)
        back = (dot_nn(dg_all, wg) + dot_nn(du_all, wu)).astype(BF16)
        back = jnp.concatenate([back, jnp.pad(grads, ((0, 0), (0, pad))).astype(BF16)], 1)
        back_sum = lax.psum_scatter(back, "dp", scatter_dimension=0, tiled=True)
    back_own = lax.psum(back_sum, "tensor").astype(F32)

    if eight:
        mix_sum = scatter_eight([after(m, back_sum) for m in mix])
        (down_grad,) = weight_grads(dy_chunks, [hg], width)
        gate_grad_w, up_grad_w = weight_grads(x_chunks, [dg, du], width)
        back_own = after(back_own, mix_sum, down_grad, gate_grad_w, up_grad_w)
    else:
        mix = dot_nn(hg_all, wd).astype(BF16)
        mix_sum = lax.psum_scatter(mix, "dp", scatter_dimension=0, tiled=True)
        down_grad = dot_tn(hg_all, dy_all)
        gate_grad_w = dot_tn(dg_all, x_all)
        up_grad_w = dot_tn(du_all, x_all)
    mine = (jnp.arange(tokens, dtype=jnp.int32) // part == t_index)[:, None]
    mix_sum = (mix_sum.astype(F32) + jnp.where(mine, middle, 0.0)).astype(BF16)
    down_grad = down_grad.reshape(experts_dev, hidden_dev, width)
    gate_grad_w = gate_grad_w.reshape(experts_dev, hidden_dev, width).transpose(0, 2, 1)
    up_grad_w = up_grad_w.reshape(experts_dev, hidden_dev, width).transpose(0, 2, 1)

    ffn_back = back_own[:, :width]
    gate_grad = back_own[:, width : width + num_experts]
    select_grad = (gate_grad - jnp.sum(gate_grad * gate_own, axis=-1, keepdims=True)) / total_own
    prob_grad = mask_own * select_grad
    logit_grad = (
        prob * (prob_grad - jnp.sum(prob_grad * prob, axis=-1, keepdims=True))
    ).astype(BF16)
    ffn_grad = ffn_back + dot_nt(logit_grad, router_weight)
    ffn_gain_part = jnp.sum(ffn_grad * normed_two, axis=0)
    mid_grad = out_grad.astype(F32) + norm_reverse(ffn_grad * ffn_gain, normed_two, scale_two)
    mid_rows = mid_grad.astype(BF16)
    block_output = lax.psum(after(mix_sum, mid_rows), "tensor")

    d_attn = dot_nn(mid_rows, output_projection).astype(BF16)
    d_out = d_attn.reshape(tokens, kv, group, head_dim)
    delta = jnp.sum(d_out.astype(F32) * attn_out.astype(F32), axis=-1)
    delta = jnp.transpose(delta, (1, 2, 0))[..., None]
    v_grad = jnp.einsum("kgqs,qkgd->skd", probs_b, d_out, preferred_element_type=F32)
    p_grad = jnp.einsum("qkgd,skd->kgqs", d_out, v_rows, preferred_element_type=F32)
    s_grad = (probs * (p_grad - delta) * scale_value).astype(BF16)
    q_grad = jnp.einsum("kgqs,skd->qkgd", s_grad, k_rot, preferred_element_type=F32)
    k_grad = jnp.einsum("kgqs,qkgd->skd", s_grad, q_rot, preferred_element_type=F32)
    q_back = rope_back(q_grad.reshape(tokens, heads, head_dim), cos_rows, sin_rows)
    q_gain_part = jnp.sum(q_back * q_hat, axis=(0, 1))
    q_raw_grad = norm_reverse(q_back * query_norm_gain, q_hat, q_scale).astype(BF16)
    q_raw_grad = q_raw_grad.reshape(tokens, -1)
    k_back = rope_back(k_grad, cos_rows, sin_rows)
    k_gain_part = jnp.sum(k_back * k_hat, axis=(0, 1))
    k_raw_grad = norm_reverse(k_back * key_norm_gain, k_hat, k_scale).astype(BF16)
    k_raw_grad = k_raw_grad.reshape(tokens, -1)
    v_grad_b = v_grad.astype(BF16).reshape(tokens, -1)

    in_f = (
        dot_nt(q_raw_grad, query_weight)
        + dot_nt(k_raw_grad, key_projection)
        + dot_nt(v_grad_b, value_projection)
    )
    in_part = in_f.astype(BF16)
    attn_in_grad = scatter_z(in_part, t_index, n_t)
    normed_own = row_block(normed_one, t_index, n_t)
    scale_own = row_block(scale_one, t_index, n_t)
    mid_own = row_block(mid_grad, t_index, n_t)
    input_own = mid_own + norm_reverse(attn_in_grad * attn_gain, normed_own, scale_own)
    input_grad = gather_z(input_own.astype(BF16), t_index, n_t)
    block_output = after(block_output, input_own)

    attn_gain_part = jnp.sum(in_f * normed_one, axis=0)
    extra = 8
    cols = q_cols + 2 * kv_cols + num_experts + pad
    gains = jnp.concatenate([attn_gain_part, ffn_gain_part / n_t, q_gain_part, k_gain_part])
    gains = jnp.pad(gains, (0, extra * cols - gains.shape[0])).reshape(extra, cols).astype(BF16)
    logit_pad = jnp.pad(logit_grad, ((0, 0), (0, pad)))
    qkv = jnp.concatenate([q_raw_grad, k_raw_grad, v_grad_b, logit_pad], 1)
    if eight:
        qkv = jnp.concatenate([qkv, gains], 0)
        qkv_chunks = gather_eight(qkv)
        attn_late = after(attn_flat, q_raw_grad)
        attn_all = lax.all_gather(attn_late, "dp", axis=0, tiled=True)
        slabs = []
        sent_in, sent_mid = lax.optimization_barrier((attn_in, mid_rows, in_part))[:2]
        for r in range(8):
            start = (d_index ^ r) * slab
            piece = jnp.concatenate(
                [lax.dynamic_slice_in_dim(a, start, slab, 1) for a in (sent_in, sent_mid)], 1
            )
            slabs.append(piece if r == 0 else swap(piece, r, 8))
        q_w, k_w, v_w, out_w, router_w, gain_sum = tail_grads(
            d_index, slabs, qkv_chunks, x_chunks, attn_all, q_cols, kv_cols
        )
        router_w = router_w[:, :num_experts]
    else:
        spread = lambda a: lax.all_to_all(a, "dp", split_axis=1, concat_axis=0, tiled=True)
        attn_all = lax.all_gather(attn_flat, "dp", axis=0, tiled=True)
        qkv_all = lax.all_gather(qkv, "dp", axis=0, tiled=True)
        qkv_w = dot_tn(spread(attn_in), qkv_all)
        q_w = qkv_w[:, :q_cols]
        k_w = qkv_w[:, q_cols : q_cols + kv_cols]
        v_w = qkv_w[:, q_cols + kv_cols : q_cols + 2 * kv_cols]
        out_w = dot_tn(spread(mid_rows), attn_all)
        x_slab = lax.dynamic_slice_in_dim(x_all, d_index * slab, slab, 1)
        router_w = dot_tn(x_slab, qkv_all[:, q_cols + 2 * kv_cols :])[:, :num_experts]
        gain_sum = lax.psum(gains.astype(F32), "dp")
    gain_flat = gain_sum.reshape(-1)

    def piece_of(start, length):
        size = length // n_dp
        return lax.dynamic_slice_in_dim(gain_flat, start + d_index * size, size, 0)

    spans = [(0, width), (width, width), (2 * width, head_dim), (2 * width + head_dim, head_dim)]
    packed = jnp.concatenate([piece_of(a, b) for a, b in spans])
    packed = jnp.pad(packed, (0, -packed.shape[0] % 1024)).reshape(-1, LANES)
    if n_t == 4:
        packed = packed + lax.ppermute(packed, "tensor", [(i, i ^ 1) for i in range(4)])
        packed = packed + lax.ppermute(packed, "tensor", [(i, i ^ 2) for i in range(4)])
    else:
        packed = lax.psum(packed, "tensor")
    packed = packed.reshape(-1)
    sizes = [b // n_dp for _, b in spans]
    starts = [sum(sizes[:i]) for i in range(4)]
    attn_gain_grad, ffn_gain_grad, q_gain_grad, k_gain_grad = [
        packed[s : s + n] for s, n in zip(starts, sizes)
    ]
    return (
        block_output,
        input_grad,
        attn_gain_grad,
        q_w,
        k_w,
        v_w,
        q_gain_grad,
        k_gain_grad,
        out_w,
        ffn_gain_grad,
        router_w,
        gate_grad_w,
        up_grad_w,
        down_grad,
    )


def solution(mesh):
    return jax.shard_map(
        local,
        mesh=mesh,
        in_specs=(
            P("dp", None),
            P("dp", None),
            P("dp", None),
            P(),
            P(None, "tensor"),
            P(None, "tensor"),
            P(None, "tensor"),
            P(),
            P(),
            P(None, "tensor"),
            P(),
            P(),
            P("dp", None, "tensor"),
            P("dp", None, "tensor"),
            P("dp", "tensor", None),
            P("dp", None),
        ),
        out_specs=(
            P("dp", None),
            P("dp", None),
            P("dp"),
            P("dp", "tensor"),
            P("dp", "tensor"),
            P("dp", "tensor"),
            P("dp"),
            P("dp"),
            P("dp", "tensor"),
            P("dp"),
            P("dp", None),
            P("dp", None, "tensor"),
            P("dp", None, "tensor"),
            P("dp", "tensor", None),
        ),
        check_vma=False,
    )
```
